256 devices in a mesh: frame: 32 (over x, z), space: 8 (over y, core).
Axes of the slice: x: 4, y: 4, z: 8, core: 2. Of those that a mesh axis runs over, the one named last changes fastest.
Arguments:
- queries: bfloat16 [128, 1024, 2240], P('frame', 'space'), may hold values from -6 to 6
- keys: bfloat16 [128, 1024, 2240], P('frame', 'space'), may hold values from -16 to 16
- values: bfloat16 [128, 1024, 2240], P('frame', 'space'), may hold values from -16 to 16
- out_weight: bfloat16 [2240, 2240], P('frame'), may hold values from -0.125 to 0.125
- conv_taps: float32 [3, 2240], replicated, may hold values from -3 to 3
Outputs:
- mixed: bfloat16 [128, 1024, 2240], P('frame', 'space')
The draws below stay inside these ranges and needn't reach their ends.
All inputs are finite; a program needn't handle non-finite values.
Results may differ from the reference program's by a relative error of at most 0.0059.
Values may be sent and summed in bfloat16 or wider, within the bound.
No kernel may reach another device: no remote copies, remote signals or barrier semaphores. Data moves between devices by JAX's collectives and lax.ppermute only.
A program may use at most 192 MiB of HBM per device.

```python
import math
import jax
import jax.numpy as jnp
from jax import lax

HEADS = 20
HEAD_DIM = 112
D = 2240
FRAMES = 128
SPATIAL = 1024


def key_value_draw(base_key):
    subkeys = jax.random.split(jax.random.fold_in(base_key, 17), 9)
    low_scale = 0.3
    high_scale = 2.0
    token_scale = jnp.exp(jax.random.uniform(subkeys[0], (FRAMES, SPATIAL, 1), jnp.float32, math.log(low_scale), math.log(high_scale)))
    head_gain = jnp.exp(jax.random.uniform(subkeys[5], (1, 1, HEADS, 1), jnp.float32, math.log(0.6), math.log(1.6)))
    channel_gain = jnp.exp(jax.random.uniform(subkeys[6], (1, 1, HEADS, HEAD_DIM), jnp.float32, math.log(0.3), math.log(3.0)))
    frame_channel_gain = jnp.exp(jax.random.uniform(subkeys[7], (FRAMES, 1, HEADS, HEAD_DIM), jnp.float32, math.log(0.6), math.log(1.6)))
    key_gains = (head_gain * channel_gain * frame_channel_gain).reshape(FRAMES, 1, D)
    raw_keys = jax.random.normal(subkeys[1], (FRAMES, SPATIAL, D), jnp.float32) * token_scale * key_gains
    keys_out = jnp.clip(raw_keys, -16.0, 16.0)
    common_mixing = jax.random.normal(subkeys[2], (1, HEADS, HEAD_DIM, HEAD_DIM), jnp.float32) * (0.35 / math.sqrt(HEAD_DIM))
    frame_mixing = jax.random.normal(subkeys[8], (FRAMES, HEADS, HEAD_DIM, HEAD_DIM), jnp.float32) / math.sqrt(HEAD_DIM)
    mixing = common_mixing + frame_mixing
    frame_gain = jnp.exp(jax.random.uniform(subkeys[3], (FRAMES, 1, 1, 1), jnp.float32, math.log(0.3), math.log(3.0)))
    key_relu = jax.nn.relu(keys_out).reshape(FRAMES, SPATIAL, HEADS, HEAD_DIM)
    signal = jnp.einsum('fshd,fhde->fshe', key_relu, mixing, precision=lax.Precision.HIGHEST) * frame_gain
    noise = 0.5 * jax.random.normal(subkeys[4], (FRAMES, SPATIAL, D), jnp.float32)
    values_out = jnp.clip(signal.reshape(FRAMES, SPATIAL, D) + noise, -16.0, 16.0)
    return (keys_out, values_out)


def draw_keys(key, part):
    return key_value_draw(key)[0].astype(jnp.bfloat16)


def draw_values(key, part):
    return key_value_draw(key)[1].astype(jnp.bfloat16)


def level_of(own_key, extent, pieces, least, high):
    def one(axis_at, parts):
        draws = jax.random.uniform(jax.random.fold_in(jax.random.fold_in(own_key, 6), axis_at), (parts,), jnp.float32, least / len(pieces), high / len(pieces))
        return jnp.repeat(jnp.exp(draws), extent[axis_at] // parts).reshape((-1,) + (1,) * (len(extent) - axis_at - 1))

    loudness = one(*pieces[0])
    for cut in pieces[1:]:
        loudness = loudness * one(*cut)
    return loudness


def scatter_about(key, shape, deviation, bound, cuts=(), kind=jnp.bfloat16):
    result = jax.random.normal(key, shape, jnp.float32) * deviation
    if len(cuts) > 0:
        result = level_of(key, shape, cuts, -0.22, 0.18) * result
    return jnp.clip(result, min=-bound, max=bound).astype(kind)


def setup_inputs(seed: int = 0) -> dict:
    key_of = jax.random.split(jax.random.key(seed), 6)
    return {
        "queries": scatter_about(key_of[0], (FRAMES, SPATIAL, D), 1.0, 6.0, ((0, 32), (1, 8))),
        "keys": draw_keys(jax.random.fold_in(key_of[5], 71), 0),
        "values": draw_values(jax.random.fold_in(key_of[5], 71), 0),
        "out_weight": scatter_about(key_of[3], (D, D), D ** -0.5, 0.125, ((0, 32),)),
        "conv_taps": scatter_about(key_of[4], (3, D), 0.6, 3.0, (), jnp.float32),
    }


stab_eps = 1e-6


def reference(queries, keys, values, out_weight, conv_taps):
    frame_count = queries.shape[0]
    spatial_count = queries.shape[1]
    key_relu = jax.nn.relu(keys.astype(jnp.float32)).reshape(frame_count, spatial_count, HEADS, HEAD_DIM)
    value_rows = values.astype(jnp.float32).reshape(frame_count, spatial_count, HEADS, HEAD_DIM)
    frame_kv = jnp.einsum("fshd,fshe->fhde", key_relu, value_rows, precision=lax.Precision.HIGHEST)
    frame_ksum = jnp.sum(key_relu, axis=1)
    states = jnp.cumsum(frame_kv, axis=0)
    norms = jnp.cumsum(frame_ksum, axis=0)
    query_relu = jax.nn.relu(queries.astype(jnp.float32)).reshape(frame_count, spatial_count, HEADS, HEAD_DIM)
    numerator = jnp.einsum("fshd,fhde->fshe", query_relu, states, precision=lax.Precision.HIGHEST)
    denominator = jnp.einsum("fshd,fhd->fsh", query_relu, norms, precision=lax.Precision.HIGHEST) + stab_eps
    attention = (numerator / denominator[..., None]).reshape(frame_count * spatial_count, D).astype(jnp.bfloat16)
    projected = jnp.dot(attention, out_weight, preferred_element_type=jnp.float32).astype(jnp.bfloat16)
    projected = projected.reshape(frame_count, spatial_count, D)
    zero_frame = jnp.zeros((1, spatial_count, D), jnp.bfloat16)
    lag_one = jnp.concatenate([zero_frame, projected[:-1]], axis=0)
    lag_two = jnp.concatenate([zero_frame, zero_frame, projected[:-2]], axis=0)
    mixed = conv_taps[0] * projected + conv_taps[1] * lag_one + conv_taps[2] * lag_two
    return mixed.astype(jnp.bfloat16)
```

```python
import functools

import jax
import jax.numpy as jnp
from jax import lax
from jax.experimental import pallas as pl
from jax.experimental.pallas import tpu as pltpu
from jax.sharding import Mesh, PartitionSpec as P

HEADS = 20
HEAD_DIM = 112
D = HEADS * HEAD_DIM
LANES = 128
HALF_HEADS = HEADS // 2
HALF_ROWS = 1152
CHUNK = 288
HALF_COLS = 1152
COL_TILE = 384

stab_eps = 1e-06


def shift(value, axis, distance, size):
    return lax.ppermute(value, axis, [(i, (i + distance) % size) for i in range(size)])


def next_section(value, size):
    return lax.ppermute(value, ("x", "z"), [(i, i + 1) for i in range(size - 1)])


def kv_kernel(core_ref, k_ref, v_ref, out_ref, acc_ref):
    frame = pl.program_id(0)
    core = core_ref[0]

    @pl.when(frame == 0)
    def _():
        acc_ref[...] = jnp.zeros_like(acc_ref)

    tokens = k_ref.shape[1]
    ones = (lax.broadcasted_iota(jnp.int32, (tokens, LANES - HEAD_DIM), 1) == 0).astype(jnp.bfloat16)
    for head in range(HEADS):
        half, inner = divmod(head, HALF_HEADS)
        lane = head * HEAD_DIM
        keys = jnp.maximum(k_ref[0, :, lane : lane + HEAD_DIM], 0)
        vals = jnp.concatenate([v_ref[0, :, lane : lane + HEAD_DIM], ones], axis=1)
        part = lax.dot_general(
            keys, vals, (((0,), (0,)), ((), ())), preferred_element_type=jnp.float32
        )
        rows = slice(inner * HEAD_DIM, (inner + 1) * HEAD_DIM)
        total = acc_ref[half, rows, :] + part
        acc_ref[half, rows, :] = total
        out_ref[half ^ core, 0, rows, :] = total.astype(out_ref.dtype)
    for half in range(2):
        rows = slice(HALF_HEADS * HEAD_DIM, HALF_ROWS)
        out_ref[half, 0, rows, :] = jnp.zeros((HALF_ROWS - HALF_HEADS * HEAD_DIM, LANES), out_ref.dtype)


def local_kv(core, keys, values):
    frames, tokens, _ = keys.shape
    spec = pl.BlockSpec((1, tokens, D), lambda f, c: (f, 0, 0))
    return pl.pallas_call(
        kv_kernel,
        out_shape=jax.ShapeDtypeStruct((2, frames, HALF_ROWS, LANES), jnp.bfloat16),
        grid_spec=pltpu.PrefetchScalarGridSpec(
            num_scalar_prefetch=1,
            grid=(frames,),
            in_specs=[spec, spec],
            out_specs=pl.BlockSpec((2, 1, HALF_ROWS, LANES), lambda f, c: (0, f, 0, 0)),
            scratch_shapes=[pltpu.VMEM((2, HALF_ROWS, LANES), jnp.float32)],
        ),
        cost_estimate=pl.CostEstimate(
            flops=2 * frames * tokens * D * LANES, bytes_accessed=3 * frames * tokens * D * 2, transcendentals=0
        ),
        name="local_kv",
    )(core, keys, values)


def scan_kernel(in_ref, out_ref):
    total = jnp.zeros(in_ref.shape[1:], jnp.float32)
    for i in range(in_ref.shape[0]):
        out_ref[i] = total.astype(out_ref.dtype)
        total = total + in_ref[i].astype(jnp.float32)


def exclusive_scan(value):
    return pl.pallas_call(
        scan_kernel,
        out_shape=jax.ShapeDtypeStruct(value.shape, jnp.bfloat16),
        name="exclusive_scan",
    )(value)


def attention_kernel(where_ref, qh_ref, q_ref, cm_ref, ct_ref, pm_ref, pt_ref, out_ref, state_ref):
    step = pl.program_id(0)
    core, row = where_ref[0], where_ref[1]

    def fill(before, within):
        for which, (p_ref, c_ref) in enumerate(((pm_ref, cm_ref), (pt_ref, ct_ref))):
            half = which ^ core
            for s in range(4):
                chunk = lax.rem(row - s + 4, 4)
                total = p_ref[s, before].astype(jnp.float32)
                if within:
                    total = total + c_ref[s, 0].astype(jnp.float32)
                start = pl.multiple_of(chunk * CHUNK, CHUNK)
                state_ref[half, pl.ds(start, CHUNK), :] = total.astype(state_ref.dtype)

    @pl.when(step == 0)
    def _():
        fill(1, False)

    @pl.when(step == 1)
    def _():
        fill(0, False)

    @pl.when(step >= 2)
    def _():
        fill(0, True)

    def heads(source):
        for head in range(HEADS):
            half, inner = divmod(head, HALF_HEADS)
            lane = head * HEAD_DIM
            query = jnp.maximum(source[0, :, lane : lane + HEAD_DIM], 0)
            state = state_ref[half, inner * HEAD_DIM : (inner + 1) * HEAD_DIM, :]
            both = jnp.dot(query, state, preferred_element_type=jnp.float32)
            scale = 1.0 / (both[:, HEAD_DIM : HEAD_DIM + 1] + stab_eps)
            out_ref[0, :, lane : lane + HEAD_DIM] = (both[:, :HEAD_DIM] * scale).astype(out_ref.dtype)

    @pl.when(step < 2)
    def _():
        heads(qh_ref)

    @pl.when(step >= 2)
    def _():
        heads(q_ref)


def attention(where, behind, queries, c_mine, c_other, p_mine, p_other):
    frames, tokens, _ = queries.shape
    halo = behind.shape[0]
    chunks = pl.BlockSpec((4, 1, CHUNK, LANES), lambda f, w: (0, jnp.maximum(f - halo, 0), 0, 0))
    whole = pl.BlockSpec((4, 2, CHUNK, LANES), lambda f, w: (0, 0, 0, 0))
    return pl.pallas_call(
        attention_kernel,
        out_shape=jax.ShapeDtypeStruct((frames + halo, tokens, D), jnp.bfloat16),
        grid_spec=pltpu.PrefetchScalarGridSpec(
            num_scalar_prefetch=1,
            grid=(frames + halo,),
            in_specs=[
                pl.BlockSpec((1, tokens, D), lambda f, w: (jnp.minimum(f, halo - 1), 0, 0)),
                pl.BlockSpec((1, tokens, D), lambda f, w: (jnp.maximum(f - halo, 0), 0, 0)),
                chunks, chunks, whole, whole,
            ],
            out_specs=pl.BlockSpec((1, tokens, D), lambda f, w: (f, 0, 0)),
            scratch_shapes=[pltpu.VMEM((2, HALF_ROWS, LANES), jnp.bfloat16)],
        ),
        cost_estimate=pl.CostEstimate(
            flops=2 * (frames + halo) * tokens * D * LANES,
            bytes_accessed=2 * (frames + halo) * tokens * D * 2,
            transcendentals=0,
        ),
        name="attention",
    )(where, behind, queries, c_mine, c_other, p_mine, p_other)


def assemble_kernel(in_ref, out_ref):
    blocks, rows, _ = in_ref.shape
    for i in range(blocks):
        out_ref[i * rows : (i + 1) * rows, :] = in_ref[i]


def assemble(blocks):
    count, rows, cols = blocks.shape
    tile = COL_TILE
    return pl.pallas_call(
        assemble_kernel,
        out_shape=jax.ShapeDtypeStruct((count * rows, cols), blocks.dtype),
        grid=(cols // tile,),
        in_specs=[pl.BlockSpec((count, rows, tile), lambda j: (0, 0, j))],
        out_specs=pl.BlockSpec((count * rows, tile), lambda j: (0, j)),
        cost_estimate=pl.CostEstimate(flops=0, bytes_accessed=4 * count * rows * cols, transcendentals=0),
        name="assemble",
    )(blocks)


def project_kernel(core_ref, att_ref, w_ref, taps_ref, *refs):
    out_ref = refs[-1]
    frames, tokens, _ = out_ref.shape
    prod = jnp.dot(att_ref[...], w_ref[...], preferred_element_type=jnp.float32)
    prod = prod.astype(jnp.bfloat16).astype(jnp.float32)
    taps = taps_ref[...]
    for f in range(frames):
        now, one, two = (prod[(f + 2 - lag) * tokens : (f + 3 - lag) * tokens] for lag in range(3))
        mixed = taps[0:1] * now + taps[1:2] * one + taps[2:3] * two
        out_ref[f] = mixed.astype(out_ref.dtype)


def project(half_of, att, weight, taps, frames, earlier=None):
    rows = att.shape[0]
    tokens = rows // (frames + 2)
    tiles = HALF_COLS // COL_TILE
    in_specs = [
        pl.BlockSpec((rows, D), lambda j, c: (0, 0)),
        pl.BlockSpec((D, COL_TILE), lambda j, c: (0, j)),
        pl.BlockSpec((3, COL_TILE), lambda j, c: (0, c[0] * tiles + j)),
    ]
    args = [half_of, att, weight, taps]
    aliases = {}
    if earlier is not None:
        in_specs.append(pl.BlockSpec(memory_space=pl.ANY))
        args.append(earlier)
        aliases = {4: 0}
    return pl.pallas_call(
        project_kernel,
        out_shape=jax.ShapeDtypeStruct((frames, tokens, D), jnp.bfloat16),
        grid_spec=pltpu.PrefetchScalarGridSpec(
            num_scalar_prefetch=1,
            grid=(tiles,),
            in_specs=in_specs,
            out_specs=pl.BlockSpec((frames, tokens, COL_TILE), lambda j, c: (0, 0, c[0] * tiles + j)),
        ),
        input_output_aliases=aliases,
        cost_estimate=pl.CostEstimate(
            flops=2 * rows * D * HALF_COLS, bytes_accessed=2 * D * (HALF_COLS + rows), transcendentals=0
        ),
        name="project",
    )(*args)


def gather_weight(weight, core):
    padded = jnp.pad(weight, ((0, 0), (0, 2 * HALF_COLS - D)))
    mine = lax.dynamic_slice_in_dim(padded, core * HALF_COLS, HALF_COLS, axis=1)
    return lax.all_gather(mine, ("x", "z"), axis=0)


def per_device(queries, keys, values, out_weight, conv_taps):
    frames, tokens, _ = queries.shape
    nx, nz, ny = lax.axis_size("x"), lax.axis_size("z"), lax.axis_size("y")
    sections = nx * nz
    core, row = lax.axis_index("c"), lax.axis_index("y")

    behind = next_section(queries[frames - 2 :], sections)
    weight_blocks = gather_weight(out_weight, core)

    sums = local_kv(jnp.reshape(core, (1,)), keys, values)
    chip = sums[0].astype(jnp.float32) + shift(sums[1], "c", 1, 2).astype(jnp.float32)

    def chunk_of(value, index):
        return lax.dynamic_slice_in_dim(value, index * CHUNK, CHUNK, axis=value.ndim - 2)

    def scatter_y(value):
        total = chunk_of(value, row)
        for s in range(1, ny):
            piece = chunk_of(value, lax.rem(row + s, ny)).astype(jnp.bfloat16)
            total = total + shift(piece, "y", s, ny).astype(jnp.float32)
        return total

    last = scatter_y(chip[frames - 1])
    rest = scatter_y(chip[: frames - 1])

    pieces = last.reshape(sections, CHUNK // sections, LANES).astype(jnp.bfloat16)
    pieces = lax.all_to_all(pieces, ("x", "z"), 0, 0)
    before = lax.all_to_all(exclusive_scan(pieces), ("x", "z"), 0, 0).reshape(CHUNK, LANES)
    tail = next_section((last - rest[frames - 2]).astype(jnp.bfloat16), sections)

    def gather_y(value):
        return jnp.stack([value] + [shift(value, "y", s, ny) for s in range(1, ny)])

    c_mine = gather_y(jnp.concatenate([rest, last[None]]).astype(jnp.bfloat16))
    c_other = shift(c_mine, "c", 1, 2)
    before2 = (before.astype(jnp.float32) - tail.astype(jnp.float32)).astype(jnp.bfloat16)
    p_mine = gather_y(jnp.stack([before, before2]))
    p_other = shift(p_mine, "c", 1, 2)

    att = attention(jnp.stack([core, row]), behind, queries, c_mine, c_other, p_mine, p_other)
    att = att.reshape((frames + 2) * tokens, D)

    w_mine = assemble(weight_blocks)
    w_other = shift(w_mine, "c", 1, 2)
    out = project(jnp.reshape(core, (1,)), att, w_mine, conv_taps, frames)
    return project(jnp.reshape(1 - core, (1,)), att, w_other, conv_taps, frames, out)


def solution(mesh):
    fine = Mesh(mesh.devices.reshape(4, 8, 4, 2), ("x", "z", "y", "c"))
    in_specs = (
        P(("x", "z"), ("y", "c"), None),
        P(("x", "z"), ("y", "c"), None),
        P(("x", "z"), ("y", "c"), None),
        P(("x", "z"), None),
        P(),
    )
    return jax.shard_map(
        per_device, mesh=fine, in_specs=in_specs, out_specs=in_specs[0], check_vma=False
    )
```

```python
import functools

import jax
import jax.numpy as jnp
from jax import lax
from jax.experimental import pallas as pl
from jax.experimental.pallas import tpu as pltpu
from jax.sharding import Mesh, PartitionSpec as P


HEADS = 20
HEAD_DIM = 112
D = HEADS * HEAD_DIM
LANES = 128
HALF_HEADS = HEADS // 2
HALF_ROWS = 1152
BLOCK, PADDED = 70, 72
PAIR = 2 * PADDED
CHUNK = 288
HALF_COLS = 1152
COL_TILE = 384

stab_eps = 1e-06


def shift(value, axis, distance, size):
    return lax.ppermute(value, axis, [(i, (i + distance) % size) for i in range(size)])


def next_section(value, size):
    return lax.ppermute(value, ("x", "z"), [(i, i + 1) for i in range(size - 1)])


def after(value, *others):
    return lax.optimization_barrier((value,) + others)[0]


def kv_kernel(core_ref, k_ref, v_ref, mine_ref, theirs_ref, acc_ref):
    frame = pl.program_id(0)
    core = core_ref[0]

    @pl.when(frame == 0)
    def _():
        acc_ref[...] = jnp.zeros_like(acc_ref)

    tokens = k_ref.shape[2]
    pad = jnp.zeros((LANES - HEAD_DIM, tokens), jnp.bfloat16)
    ones = (lax.broadcasted_iota(jnp.int32, (LANES, tokens), 0) == HEAD_DIM).astype(jnp.bfloat16)
    for head in range(HEADS):
        half, inner = divmod(head, HALF_HEADS)
        keys = jnp.maximum(k_ref[0, head * HEAD_DIM : (head + 1) * HEAD_DIM, :], 0)
        vals = v_ref[0, head * HEAD_DIM : (head + 1) * HEAD_DIM, :]
        left = jnp.concatenate([vals, keys], axis=1)
        right = jnp.concatenate([jnp.concatenate([keys, pad], axis=0), ones], axis=1)
        part = lax.dot_general(
            left, right, (((1,), (1,)), ((), ())), preferred_element_type=jnp.float32
        )
        rows = slice(inner * HEAD_DIM, (inner + 1) * HEAD_DIM)
        acc_ref[half, rows, :] = acc_ref[half, rows, :] + part
    norm = lax.broadcasted_iota(jnp.int32, (PADDED, LANES), 1) == HEAD_DIM
    for ref, half in ((mine_ref, core), (theirs_ref, 1 - core)):
        for pair in range(HALF_ROWS // PAIR):
            cuts = [
                jnp.where(norm, acc_ref[half, b * PADDED : (b + 1) * PADDED, :], acc_ref[half, b * BLOCK : b * BLOCK + PADDED, :])
                for b in (2 * pair, 2 * pair + 1)
            ]
            ref[0, pair * PAIR : (pair + 1) * PAIR, :] = jnp.concatenate(cuts, axis=0).astype(ref.dtype)


def limit(mib):
    return pltpu.CompilerParams(vmem_limit_bytes=mib << 20)


def local_kv(core, keys, values):
    frames, _, tokens = keys.shape
    spec = pl.BlockSpec((1, D, tokens), lambda f, c: (f, 0, 0))
    out = pl.BlockSpec((1, HALF_ROWS, LANES), lambda f, c: (f, 0, 0))
    return pl.pallas_call(
        kv_kernel,
        out_shape=[jax.ShapeDtypeStruct((frames, HALF_ROWS, LANES), jnp.bfloat16)] * 2,
        grid_spec=pltpu.PrefetchScalarGridSpec(
            num_scalar_prefetch=1,
            grid=(frames,),
            in_specs=[spec, spec],
            out_specs=[out, out],
            scratch_shapes=[pltpu.VMEM((2, HALF_ROWS, LANES), jnp.float32)],
        ),
        compiler_params=limit(60),
        cost_estimate=pl.CostEstimate(
            flops=4 * frames * tokens * D * LANES, bytes_accessed=4 * frames * tokens * D * 2, transcendentals=0
        ),
        name="local_kv",
    )(core, keys, values)


def copy_kernel(in_ref, out_ref):
    out_ref[...] = in_ref[...]


def last_two(queries):
    frames, _, tokens = queries.shape
    return pl.pallas_call(
        copy_kernel,
        out_shape=jax.ShapeDtypeStruct((2, D, tokens), queries.dtype),
        grid=(4,),
        in_specs=[pl.BlockSpec((1, D // 2, tokens), lambda i: (frames - 2 + i // 2, i % 2, 0))],
        out_specs=pl.BlockSpec((1, D // 2, tokens), lambda i: (i // 2, i % 2, 0)),
        compiler_params=limit(60),
        name="last_two",
    )(queries)


def split_kernel(row_ref, mine_ref, other_ref, own_ref, *piece_refs):
    frames = mine_ref.shape[0]
    for s in range(4):
        rows = pl.ds(pl.multiple_of(lax.rem(row_ref[0] + s, 4) * CHUNK, CHUNK), CHUNK)
        for f in range(frames):
            total = mine_ref[f, rows, :].astype(jnp.float32) + other_ref[f, rows, :].astype(jnp.float32)
            if s == 0:
                own_ref[f] = total
            elif f >= frames - 2:
                piece_refs[s - 1][f - frames + 2] = total.astype(jnp.bfloat16)
            else:
                piece_refs[s + 2][f] = total.astype(jnp.bfloat16)


def split(row, mine, other):
    frames = mine.shape[0]
    vmem = pl.BlockSpec(memory_space=pltpu.VMEM)
    return pl.pallas_call(
        split_kernel,
        out_shape=[jax.ShapeDtypeStruct((frames, CHUNK, LANES), jnp.float32)]
        + [jax.ShapeDtypeStruct((2, CHUNK, LANES), jnp.bfloat16)] * 3
        + [jax.ShapeDtypeStruct((frames - 2, CHUNK, LANES), jnp.bfloat16)] * 3,
        in_specs=[pl.BlockSpec(memory_space=pltpu.SMEM), vmem, vmem],
        out_specs=[vmem] * 7,
        compiler_params=limit(8),
        name="split",
    )(row, mine, other)


def total_kernel(own_ref, a_ref, b_ref, c_ref, sums_ref, pieces_ref):
    frames = own_ref.shape[0]
    count, rows, _ = pieces_ref.shape
    rows //= 2
    kept = []
    for f in range(2):
        total = own_ref[frames - 2 + f]
        for ref in (a_ref, b_ref, c_ref):
            total = total + ref[f].astype(jnp.float32)
        sums_ref[f] = total.astype(sums_ref.dtype)
        kept.append(total)
    earlier, last = kept
    for i in range(count):
        cut = slice(i * rows, (i + 1) * rows)
        both = jnp.concatenate([last[cut], earlier[cut]], axis=0)
        pieces_ref[i] = both.astype(pieces_ref.dtype)


def total(own, received, sections):
    vmem = pl.BlockSpec(memory_space=pltpu.VMEM)
    return pl.pallas_call(
        total_kernel,
        out_shape=[
            jax.ShapeDtypeStruct((2,) + own.shape[1:], jnp.bfloat16),
            jax.ShapeDtypeStruct((sections, 2 * CHUNK // sections, LANES), jnp.bfloat16),
        ],
        in_specs=[vmem] * 4,
        out_specs=[vmem] * 2,
        compiler_params=limit(8),
        name="total",
    )(own, *received)


def rest_kernel(own_ref, a_ref, b_ref, c_ref, last_ref, sums_ref):
    first = a_ref.shape[0]
    for f in range(first):
        total = own_ref[f]
        for ref in (a_ref, b_ref, c_ref):
            total = total + ref[f].astype(jnp.float32)
        sums_ref[f] = total.astype(sums_ref.dtype)
    for f in range(2):
        sums_ref[first + f] = last_ref[f]


def rest(own, received, last):
    vmem = pl.BlockSpec(memory_space=pltpu.VMEM)
    return pl.pallas_call(
        rest_kernel,
        out_shape=jax.ShapeDtypeStruct(own.shape, jnp.bfloat16),
        in_specs=[vmem] * 5,
        out_specs=vmem,
        compiler_params=limit(8),
        name="rest",
    )(own, *received, last)


def scan_kernel(in_ref, out_ref):
    count, rows, lanes = in_ref.shape
    rows //= 2
    before = jnp.zeros((rows, lanes), jnp.float32)
    before2 = before
    for i in range(count):
        out_ref[i] = jnp.concatenate([before, before2], axis=0).astype(out_ref.dtype)
        here = in_ref[i].astype(jnp.float32)
        before, before2 = before + here[:rows], before + here[rows:]


def exclusive_scan(value):
    vmem = pl.BlockSpec(memory_space=pltpu.VMEM)
    return pl.pallas_call(
        scan_kernel,
        out_shape=jax.ShapeDtypeStruct(value.shape, value.dtype),
        in_specs=[vmem],
        out_specs=vmem,
        compiler_params=limit(8),
        name="exclusive_scan",
    )(value)


def join_kernel(in_ref, out_ref):
    count, rows, _ = in_ref.shape
    rows //= 2
    pieces = [in_ref[i].astype(jnp.float32) for i in range(count)]
    for k in range(2):
        whole = jnp.concatenate([p[k * rows : (k + 1) * rows] for p in pieces], axis=0)
        out_ref[k] = whole.astype(out_ref.dtype)


def join(value):
    vmem = pl.BlockSpec(memory_space=pltpu.VMEM)
    return pl.pallas_call(
        join_kernel,
        out_shape=jax.ShapeDtypeStruct((2, CHUNK, LANES), value.dtype),
        in_specs=[vmem],
        out_specs=vmem,
        compiler_params=limit(8),
        name="join",
    )(value)


def pair_kernel(place_ref, mine_ref, other_ref, out_ref):
    @pl.when(place_ref[1] % 2 == 0)
    def _():
        out_ref[:PADDED] = mine_ref[...]
        out_ref[PADDED:] = other_ref[...]

    @pl.when(place_ref[1] % 2 == 1)
    def _():
        out_ref[:PADDED] = other_ref[...]
        out_ref[PADDED:] = mine_ref[...]


def in_order(place, mine, other):
    vmem = pl.BlockSpec(memory_space=pltpu.VMEM)
    return pl.pallas_call(
        pair_kernel,
        out_shape=jax.ShapeDtypeStruct((PAIR,) + mine.shape[1:], mine.dtype),
        in_specs=[pl.BlockSpec(memory_space=pltpu.SMEM), vmem, vmem],
        out_specs=vmem,
        compiler_params=limit(8),
        name="in_order",
    )(place, mine, other)


def pack_kernel(*refs):
    for i, ref in enumerate(refs[:-1]):
        refs[-1][i] = ref[...]


def pack(arrays):
    vmem = pl.BlockSpec(memory_space=pltpu.VMEM)
    return pl.pallas_call(
        pack_kernel,
        out_shape=jax.ShapeDtypeStruct((len(arrays),) + arrays[0].shape, arrays[0].dtype),
        in_specs=[vmem] * len(arrays),
        out_specs=vmem,
        compiler_params=limit(8),
        name="pack",
    )(*arrays)


def padded_row(row):
    return row + (PADDED - BLOCK) * (row // BLOCK)


def tail_kernel(spots, where_ref, *refs):
    qh_ref, q_ref = refs[:2]
    c_refs, p_refs = (refs[2:6], refs[6:10]), (refs[10:14], refs[14:18])
    count = len(spots)
    w_refs = (refs[18 : 18 + count], refs[18 + count : 18 + 2 * count])
    taps_ref, out_ref, state_ref, att_ref, weight_ref, sem = refs[18 + 2 * count :]
    step = pl.program_id(0)
    core, row = where_ref[0], where_ref[1]
    frames, width, tokens = out_ref.shape
    steps = frames + 2

    def copies():
        made = []
        for which in range(2):
            column = pl.multiple_of((which ^ core) * HALF_COLS, HALF_COLS)
            for group, places in zip(w_refs[which], spots):
                for i, (dx, dz) in enumerate(places):
                    x = lax.rem(where_ref[2] - dx + 8, 4)
                    z = lax.rem(where_ref[3] // 2 - dz + 8, 4)
                    start = pl.multiple_of((x * 4 + z) * PAIR, PAIR)
                    target = weight_ref.at[pl.ds(start, PAIR), pl.ds(column, HALF_COLS)]
                    source = group if len(places) == 1 else group.at[i]
                    made.append(pltpu.make_async_copy(source, target, sem.at[len(made)]))
        return made

    @pl.when(step == 0)
    def _():
        for copy in copies():
            copy.start()

    def fill(before, within):
        for which in range(2):
            half = which ^ core
            for s in range(4):
                chunk = lax.rem(row - s + 4, 4)
                state = p_refs[which][s][before]
                if within:
                    state = state.astype(jnp.float32) + c_refs[which][s][0].astype(jnp.float32)
                start = pl.multiple_of(chunk * CHUNK, CHUNK)
                state_ref[half, pl.ds(start, CHUNK), :] = state.astype(state_ref.dtype)

    @pl.when(step == 0)
    def _():
        fill(1, False)

    @pl.when(step == 1)
    def _():
        fill(0, False)

    @pl.when((step >= 2) & (step < steps))
    def _():
        fill(0, True)

    def heads(source):
        pad = jnp.zeros((LANES - HEAD_DIM, tokens), jnp.bfloat16)
        lanes = pl.ds(pl.multiple_of(step * tokens, tokens), tokens)
        for head in range(HEADS):
            half, inner = divmod(head, HALF_HEADS)
            query = jnp.maximum(source[0, head * HEAD_DIM : (head + 1) * HEAD_DIM, :], 0)
            first = padded_row(inner * HEAD_DIM)
            low = first // 16 * 16
            high = -(-(padded_row(inner * HEAD_DIM + HEAD_DIM - 1) + 1) // 16) * 16
            top = jnp.dot(
                state_ref[half, low:high, :],
                jnp.concatenate([query, pad], axis=0),
                preferred_element_type=jnp.float32,
            )
            norm = state_ref[half, inner * HEAD_DIM : (inner + 1) * HEAD_DIM, HEAD_DIM : HEAD_DIM + 1]
            bottom = norm.astype(jnp.float32) * query.astype(jnp.float32)
            bottom = jnp.sum(bottom, axis=0, keepdims=True) + stab_eps
            result = top * (1.0 / bottom)
            base = half * HALF_ROWS
            if first > low:
                held = att_ref[base + low : base + low + 16, lanes].astype(jnp.float32)
                keep = lax.broadcasted_iota(jnp.int32, (16, tokens), 0) < first - low
                att_ref[base + low : base + low + 16, lanes] = jnp.where(keep, held, result[:16]).astype(att_ref.dtype)
                att_ref[base + low + 16 : base + high, lanes] = result[16:].astype(att_ref.dtype)
            else:
                att_ref[base + low : base + high, lanes] = result.astype(att_ref.dtype)

    @pl.when(step < 2)
    def _():
        heads(qh_ref)

    @pl.when((step >= 2) & (step < steps))
    def _():
        heads(q_ref)

    @pl.when(step == steps)
    def _():
        for copy in copies():
            copy.wait()

    @pl.when(step >= steps)
    def _():
        column = pl.ds(pl.multiple_of((step - steps) * width, width), width)
        prod = lax.dot_general(
            weight_ref[:, column], att_ref[...], (((0,), (0,)), ((), ())), preferred_element_type=jnp.float32
        )
        prod = prod.astype(jnp.bfloat16).astype(jnp.float32)
        taps = taps_ref[...].T
        for f in range(frames):
            now, one, two = (prod[:, (f + 2 - lag) * tokens : (f + 3 - lag) * tokens] for lag in range(3))
            mixed = taps[:, 0:1] * now + taps[:, 1:2] * one + taps[:, 2:3] * two
            out_ref[f] = mixed.astype(out_ref.dtype)


def tail(where, behind, queries, c_mine, c_other, p_mine, p_other, groups, groups_other, spots, taps):
    frames, _, tokens = queries.shape
    steps = frames + 2
    own = lambda f, w: (jnp.clip(f - 2, 0, frames - 1), 0, 0)
    tile = lambda f: jnp.maximum(f - steps, 0)
    chunk = pl.BlockSpec((1, CHUNK, LANES), own)
    whole = pl.BlockSpec((2, CHUNK, LANES), lambda f, w: (0, 0, 0))
    pairs = sum(len(places) for places in spots)
    return pl.pallas_call(
        functools.partial(tail_kernel, spots),
        out_shape=jax.ShapeDtypeStruct((frames, D, tokens), jnp.bfloat16),
        grid_spec=pltpu.PrefetchScalarGridSpec(
            num_scalar_prefetch=1,
            grid=(steps + 2 * HALF_COLS // COL_TILE,),
            in_specs=[
                pl.BlockSpec((1, D, tokens), lambda f, w: (jnp.minimum(f, 1), 0, 0)),
                pl.BlockSpec((1, D, tokens), own),
            ]
            + [chunk] * 8
            + [whole] * 8
            + [pl.BlockSpec(memory_space=pl.ANY)] * (2 * len(groups))
            + [pl.BlockSpec((3, COL_TILE), lambda f, w: (0, tile(f)))],
            out_specs=pl.BlockSpec((frames, COL_TILE, tokens), lambda f, w: (0, tile(f), 0)),
            scratch_shapes=[
                pltpu.VMEM((2, HALF_ROWS, LANES), jnp.bfloat16),
                pltpu.VMEM((2 * HALF_ROWS, steps * tokens), jnp.bfloat16),
                pltpu.VMEM((2 * HALF_ROWS, 2 * HALF_COLS), jnp.bfloat16),
                pltpu.SemaphoreType.DMA((2 * pairs,)),
            ],
        ),
        compiler_params=limit(40),
        cost_estimate=pl.CostEstimate(
            flops=2 * steps * tokens * D * (D + LANES), bytes_accessed=2 * D * D, transcendentals=0
        ),
        name="tail",
    )(where, behind, queries, *c_mine, *c_other, *p_mine, *p_other, *groups, *groups_other, taps)


def layer(queries, keys, values, out_weight, conv_taps):
    nx, nz, ny = lax.axis_size("x"), lax.axis_size("z"), lax.axis_size("y")
    sections = nx * nz
    core, row = lax.axis_index("c"), lax.axis_index("y")
    place = jnp.stack([lax.axis_index("x"), lax.axis_index("z")])
    where = jnp.stack([core, row, lax.axis_index("x"), lax.axis_index("z")])
    queries, keys, values = (jnp.transpose(a, (0, 2, 1)) for a in (queries, keys, values))

    def along_y(value):
        return [shift(value, "y", s, ny) for s in range(1, ny)]

    def to_partner(arrays):
        return [shift(value, "c", 1, 2) for value in arrays]

    rows, cols = out_weight.shape
    padded = jnp.pad(out_weight, ((0, PADDED - rows), (0, 2 * HALF_COLS - cols)))
    block = lax.dynamic_slice_in_dim(padded, core * HALF_COLS, HALF_COLS, axis=1)
    partner = lax.ppermute(block, "z", [(i, i ^ 1) for i in range(nz)])
    behind = next_section(last_two(queries), sections)
    mine, theirs = local_kv(jnp.reshape(core, (1,)), keys, values)
    theirs = shift(theirs, "c", 1, 2)
    pair = in_order(place, block, after(partner, mine))
    above, below = shift(pair, "z", 2, nz), shift(pair, "z", -2, nz)
    pair_up, pair_down = shift(pair, "x", 1, nx), shift(pair, "x", -1, nx)
    own, *pieces = split(jnp.reshape(row, (1,)), mine, theirs)
    received = [shift(pieces[s - 1], "y", s, ny) for s in range(1, ny)]

    last, cuts = total(own, received, sections)
    cuts = lax.all_to_all(cuts, ("x", "z"), 0, 0)

    below = after(below, last)
    far = shift(below, "z", -2, nz)
    below_up, below_down = shift(below, "x", 1, nx), shift(below, "x", -1, nx)
    received = [shift(after(pieces[s + 2], last), "y", s, ny) for s in range(1, ny)]
    cuts = exclusive_scan(cuts)
    before = lax.all_to_all(cuts, ("x", "z"), 0, 0)
    both = pack([after(above, cuts), after(far, cuts)])
    both_up, both_down = shift(both, "x", 1, nx), shift(both, "x", -1, nx)
    sums = rest(own, [after(r, cuts) for r in received], last)
    c_mine = [sums] + along_y(sums)
    pair_two = shift(after(pair_down, cuts), "x", -1, nx)
    below_two = shift(after(below_down, cuts), "x", -1, nx)
    early = to_partner([after(a, cuts) for a in (pair, below, both, pair_up, pair_down, below_up, below_down)])

    before = join(before)
    p_mine = [before] + along_y(before)
    both_two = shift(after(both_up, before), "x", 1, nx)
    c_other = to_partner([after(a, before) for a in c_mine])
    p_other = to_partner(p_mine)
    late = to_partner([after(a, before) for a in (both_up, both_down, pair_two, below_two, both_two)])

    here, under, others = (0,), (-1,), (1, -2)
    spots = [
        [(dx, dz) for dz in steps]
        for dx, steps in (
            (0, here), (0, under), (0, others), (1, here), (-1, here), (1, under), (-1, under),
            (1, others), (-1, others), (-2, here), (-2, under), (2, others),
        )
    ]
    groups = [pair, below, both, pair_up, pair_down, below_up, below_down, both_up, both_down, pair_two, below_two, both_two]
    out = tail(where, behind, queries, c_mine, c_other, p_mine, p_other, groups, early + late, spots, conv_taps)
    return jnp.transpose(out, (0, 2, 1))


def solution(mesh):
    fine = Mesh(mesh.devices.reshape(4, 8, 4, 2), ("x", "z", "y", "c"))
    in_specs = (
        P(("x", "z"), ("y", "c"), None),
        P(("x", "z"), ("y", "c"), None),
        P(("x", "z"), ("y", "c"), None),
        P(("x", "z"), None),
        P(),
    )
    return jax.shard_map(layer, mesh=fine, in_specs=in_specs, out_specs=in_specs[0], check_vma=False)
```

```python
import functools

import jax
import jax.numpy as jnp
from jax import lax
from jax.experimental import pallas as pl
from jax.experimental.pallas import tpu as pltpu
from jax.sharding import Mesh, PartitionSpec as P


HEADS = 20
HEAD_DIM = 112
D = HEADS * HEAD_DIM
LANES = 128
HALF_HEADS = HEADS // 2
HALF_ROWS = 1152
BLOCK, PADDED = 70, 72
PAIR = 2 * PADDED
CHUNK = 288
HALF_COLS = 1152
COL_TILE = 256

stab_eps = 1e-06


def shift(value, axis, distance, size):
    return lax.ppermute(value, axis, [(i, (i + distance) % size) for i in range(size)])


def after(value, *others):
    return lax.optimization_barrier((value,) + others)[0]


def kv_kernel(core_ref, k_ref, v_ref, mine_ref, theirs_ref, acc_ref):
    frame = pl.program_id(0)
    core = core_ref[0]

    @pl.when(frame == 0)
    def _():
        acc_ref[...] = jnp.zeros_like(acc_ref)

    tokens = k_ref.shape[2]
    pad = jnp.zeros((LANES - HEAD_DIM, tokens), jnp.bfloat16)
    ones = (lax.broadcasted_iota(jnp.int32, (LANES, tokens), 0) == HEAD_DIM).astype(jnp.bfloat16)

    @pl.loop(0, 2)
    def _(half):
        for inner in range(HALF_HEADS):
            start = half * (HALF_HEADS * HEAD_DIM) + inner * HEAD_DIM
            rows = pl.ds(pl.multiple_of(start, 16), HEAD_DIM)
            keys = jnp.maximum(k_ref[0, rows, :], 0)
            vals = v_ref[0, rows, :]
            left = jnp.concatenate([vals, keys], axis=1)
            right = jnp.concatenate([jnp.concatenate([keys, pad], axis=0), ones], axis=1)
            part = lax.dot_general(
                left, right, (((1,), (1,)), ((), ())), preferred_element_type=jnp.float32
            )
            rows = slice(inner * HEAD_DIM, (inner + 1) * HEAD_DIM)
            acc_ref[half, rows, :] = acc_ref[half, rows, :] + part

    norm = lax.broadcasted_iota(jnp.int32, (PADDED, LANES), 1) == HEAD_DIM
    for ref, half in ((mine_ref, core), (theirs_ref, 1 - core)):
        for pair in range(HALF_ROWS // PAIR):
            cuts = [
                jnp.where(norm, acc_ref[half, b * PADDED : (b + 1) * PADDED, :], acc_ref[half, b * BLOCK : b * BLOCK + PADDED, :])
                for b in (2 * pair, 2 * pair + 1)
            ]
            ref[0, pair * PAIR : (pair + 1) * PAIR, :] = jnp.concatenate(cuts, axis=0).astype(ref.dtype)


def limit(mib):
    return pltpu.CompilerParams(vmem_limit_bytes=mib << 20)


def local_kv(core, keys, values):
    frames, _, tokens = keys.shape
    spec = pl.BlockSpec((1, D, tokens), lambda f, c: (f, 0, 0))
    out = pl.BlockSpec((1, HALF_ROWS, LANES), lambda f, c: (f, 0, 0))
    return pl.pallas_call(
        kv_kernel,
        out_shape=[jax.ShapeDtypeStruct((frames, HALF_ROWS, LANES), jnp.bfloat16)] * 2,
        grid_spec=pltpu.PrefetchScalarGridSpec(
            num_scalar_prefetch=1,
            grid=(frames,),
            in_specs=[spec, spec],
            out_specs=[out, out],
            scratch_shapes=[pltpu.VMEM((2, HALF_ROWS, LANES), jnp.float32)],
        ),
        compiler_params=limit(60),
        cost_estimate=pl.CostEstimate(
            flops=4 * frames * tokens * D * LANES, bytes_accessed=4 * frames * tokens * D * 2, transcendentals=0
        ),
        name="local_kv",
    )(core, keys, values)


def split_kernel(row_ref, mine_ref, other_ref, own_ref, *piece_refs):
    frames = mine_ref.shape[0]
    for s in range(4):
        rows = pl.ds(pl.multiple_of(lax.rem(row_ref[0] + s, 4) * CHUNK, CHUNK), CHUNK)
        for f in range(frames):
            total = mine_ref[f, rows, :].astype(jnp.float32) + other_ref[f, rows, :].astype(jnp.float32)
            if s == 0:
                own_ref[f] = total
            elif f >= frames - 2:
                piece_refs[s - 1][f - frames + 2] = total.astype(jnp.bfloat16)
            else:
                piece_refs[s + 2][f] = total.astype(jnp.bfloat16)


def split(row, mine, other):
    frames = mine.shape[0]
    vmem = pl.BlockSpec(memory_space=pltpu.VMEM)
    return pl.pallas_call(
        split_kernel,
        out_shape=[jax.ShapeDtypeStruct((frames, CHUNK, LANES), jnp.float32)]
        + [jax.ShapeDtypeStruct((2, CHUNK, LANES), jnp.bfloat16)] * 3
        + [jax.ShapeDtypeStruct((frames - 2, CHUNK, LANES), jnp.bfloat16)] * 3,
        in_specs=[pl.BlockSpec(memory_space=pltpu.SMEM), vmem, vmem],
        out_specs=[vmem] * 7,
        compiler_params=limit(8),
        name="split",
    )(row, mine, other)


def total_kernel(own_ref, a_ref, b_ref, c_ref, sums_ref, pieces_ref):
    frames = own_ref.shape[0]
    count, rows, _ = pieces_ref.shape
    rows //= 2
    kept = []
    for f in range(2):
        total = own_ref[frames - 2 + f]
        for ref in (a_ref, b_ref, c_ref):
            total = total + ref[f].astype(jnp.float32)
        sums_ref[f] = total.astype(sums_ref.dtype)
        kept.append(total)
    earlier, last = kept
    for i in range(count):
        cut = slice(i * rows, (i + 1) * rows)
        both = jnp.concatenate([last[cut], earlier[cut]], axis=0)
        pieces_ref[i] = both.astype(pieces_ref.dtype)


def total(own, received, sections):
    vmem = pl.BlockSpec(memory_space=pltpu.VMEM)
    return pl.pallas_call(
        total_kernel,
        out_shape=[
            jax.ShapeDtypeStruct((2,) + own.shape[1:], jnp.bfloat16),
            jax.ShapeDtypeStruct((sections, 2 * CHUNK // sections, LANES), jnp.bfloat16),
        ],
        in_specs=[vmem] * 4,
        out_specs=[vmem] * 2,
        compiler_params=limit(8),
        name="total",
    )(own, *received)


def rest_kernel(own_ref, a_ref, b_ref, c_ref, last_ref, sums_ref):
    first = a_ref.shape[0]
    for f in range(first):
        total = own_ref[f]
        for ref in (a_ref, b_ref, c_ref):
            total = total + ref[f].astype(jnp.float32)
        sums_ref[f] = total.astype(sums_ref.dtype)
    for f in range(2):
        sums_ref[first + f] = last_ref[f]


def rest(own, received, last):
    vmem = pl.BlockSpec(memory_space=pltpu.VMEM)
    return pl.pallas_call(
        rest_kernel,
        out_shape=jax.ShapeDtypeStruct(own.shape, jnp.bfloat16),
        in_specs=[vmem] * 5,
        out_specs=vmem,
        compiler_params=limit(8),
        name="rest",
    )(own, *received, last)


def scan_kernel(in_ref, out_ref):
    count, rows, lanes = in_ref.shape
    rows //= 2
    before = jnp.zeros((rows, lanes), jnp.float32)
    before2 = before
    for i in range(count):
        out_ref[i] = jnp.concatenate([before, before2], axis=0).astype(out_ref.dtype)
        here = in_ref[i].astype(jnp.float32)
        before, before2 = before + here[:rows], before + here[rows:]


def exclusive_scan(value):
    vmem = pl.BlockSpec(memory_space=pltpu.VMEM)
    return pl.pallas_call(
        scan_kernel,
        out_shape=jax.ShapeDtypeStruct(value.shape, value.dtype),
        in_specs=[vmem],
        out_specs=vmem,
        compiler_params=limit(8),
        name="exclusive_scan",
    )(value)


def join_kernel(in_ref, out_ref):
    count, rows, _ = in_ref.shape
    rows //= 2
    pieces = [in_ref[i].astype(jnp.float32) for i in range(count)]
    for k in range(2):
        whole = jnp.concatenate([p[k * rows : (k + 1) * rows] for p in pieces], axis=0)
        out_ref[k] = whole.astype(out_ref.dtype)


def join(value):
    vmem = pl.BlockSpec(memory_space=pltpu.VMEM)
    return pl.pallas_call(
        join_kernel,
        out_shape=jax.ShapeDtypeStruct((2, CHUNK, LANES), value.dtype),
        in_specs=[vmem],
        out_specs=vmem,
        compiler_params=limit(8),
        name="join",
    )(value)


def pair_kernel(place_ref, mine_ref, other_ref, out_ref):
    @pl.when(place_ref[1] % 2 == 0)
    def _():
        out_ref[:PADDED] = mine_ref[...]
        out_ref[PADDED:] = other_ref[...]

    @pl.when(place_ref[1] % 2 == 1)
    def _():
        out_ref[:PADDED] = other_ref[...]
        out_ref[PADDED:] = mine_ref[...]


def in_order(place, mine, other):
    vmem = pl.BlockSpec(memory_space=pltpu.VMEM)
    return pl.pallas_call(
        pair_kernel,
        out_shape=jax.ShapeDtypeStruct((PAIR,) + mine.shape[1:], mine.dtype),
        in_specs=[pl.BlockSpec(memory_space=pltpu.SMEM), vmem, vmem],
        out_specs=vmem,
        compiler_params=limit(8),
        name="in_order",
    )(place, mine, other)


def pack_kernel(*refs):
    for i, ref in enumerate(refs[:-1]):
        refs[-1][i] = ref[...]


def pack(arrays):
    vmem = pl.BlockSpec(memory_space=pltpu.VMEM)
    return pl.pallas_call(
        pack_kernel,
        out_shape=jax.ShapeDtypeStruct((len(arrays),) + arrays[0].shape, arrays[0].dtype),
        in_specs=[vmem] * len(arrays),
        out_specs=vmem,
        compiler_params=limit(8),
        name="pack",
    )(*arrays)


def padded_row(row):
    return row + (PADDED - BLOCK) * (row // BLOCK)


def tail_kernel(spots, where_ref, *refs):
    qh_ref, q_ref = refs[:2]
    c_refs, p_refs = (refs[2:6], refs[6:10]), (refs[10:14], refs[14:18])
    count = len(spots)
    w_refs = (refs[18 : 18 + count], refs[18 + count : 18 + 2 * count])
    taps_ref, out_ref, state_ref, query_ref, att_ref, weight_ref, sem = refs[18 + 2 * count :]
    step = pl.program_id(0)
    core, row = where_ref[0], where_ref[1]
    frames, width, tokens = out_ref.shape
    steps = frames + 2

    def copies():
        made = []
        for which in range(2):
            column = pl.multiple_of((which ^ core) * HALF_COLS, HALF_COLS)
            for group, places in zip(w_refs[which], spots):
                for i, (dx, dz) in enumerate(places):
                    x = lax.rem(where_ref[2] - dx + 8, 4)
                    z = lax.rem(where_ref[3] // 2 - dz + 8, 4)
                    start = pl.multiple_of((x * 4 + z) * PAIR, PAIR)
                    target = weight_ref.at[pl.ds(start, PAIR), pl.ds(column, HALF_COLS)]
                    source = group if len(places) == 1 else group.at[i]
                    made.append(pltpu.make_async_copy(source, target, sem.at[len(made)]))
        return made

    @pl.when(step == 0)
    def _():
        for copy in copies():
            copy.start()

    @pl.when(step < steps)
    def _():
        before = jnp.where(step == 0, 1, 0)
        within = jnp.where(step >= 2, 1.0, 0.0)
        for which in range(2):
            half = which ^ core
            for s in range(4):
                chunk = lax.rem(row - s + 4, 4)
                state = p_refs[which][s][before].astype(jnp.float32)
                state = state + c_refs[which][s][0].astype(jnp.float32) * within
                start = pl.multiple_of(chunk * CHUNK, CHUNK)
                state_ref[half, pl.ds(start, CHUNK), :] = state.astype(state_ref.dtype)

    @pl.when(step < 2)
    def _():
        query_ref[...] = jnp.maximum(qh_ref[0], 0)

    @pl.when((step >= 2) & (step < steps))
    def _():
        query_ref[...] = jnp.maximum(q_ref[0], 0)

    @pl.when(step < steps)
    def _():
        pad = jnp.zeros((LANES - HEAD_DIM, tokens), jnp.bfloat16)
        lanes = pl.ds(pl.multiple_of(step * tokens, tokens), tokens)

        @pl.loop(0, 2)
        def _(half):
            for inner in range(HALF_HEADS):
                start = half * (HALF_HEADS * HEAD_DIM) + inner * HEAD_DIM
                query = query_ref[pl.ds(pl.multiple_of(start, 16), HEAD_DIM), :]
                first = padded_row(inner * HEAD_DIM)
                low = first // 16 * 16
                high = -(-(padded_row(inner * HEAD_DIM + HEAD_DIM - 1) + 1) // 16) * 16
                top = jnp.dot(
                    state_ref[half, low:high, :],
                    jnp.concatenate([query, pad], axis=0),
                    preferred_element_type=jnp.float32,
                )
                norm = state_ref[half, inner * HEAD_DIM : (inner + 1) * HEAD_DIM, HEAD_DIM : HEAD_DIM + 1]
                bottom = norm.astype(jnp.float32) * query.astype(jnp.float32)
                bottom = jnp.sum(bottom, axis=0, keepdims=True) + stab_eps
                result = top * (1.0 / bottom)
                base = pl.multiple_of(half * HALF_ROWS + low, 16)
                if first > low:
                    edge = pl.ds(base, 16)
                    held = att_ref[edge, lanes].astype(jnp.float32)
                    keep = lax.broadcasted_iota(jnp.int32, (16, tokens), 0) < first - low
                    att_ref[edge, lanes] = jnp.where(keep, held, result[:16]).astype(att_ref.dtype)
                    inside = pl.ds(pl.multiple_of(base + 16, 16), high - low - 16)
                    att_ref[inside, lanes] = result[16:].astype(att_ref.dtype)
                else:
                    att_ref[pl.ds(base, high - low), lanes] = result.astype(att_ref.dtype)

    @pl.when(step == steps)
    def _():
        for copy in copies():
            copy.wait()

    @pl.when(step >= steps)
    def _():
        column = pl.ds(pl.multiple_of((step - steps) * width, width), width)
        prod = lax.dot_general(
            weight_ref[:, column], att_ref[...], (((0,), (0,)), ((), ())), preferred_element_type=jnp.float32
        )
        prod = prod.astype(jnp.bfloat16).astype(jnp.float32)
        taps = taps_ref[...].T
        for f in range(frames):
            now, one, two = (prod[:, (f + 2 - lag) * tokens : (f + 3 - lag) * tokens] for lag in range(3))
            mixed = taps[:, 0:1] * now + taps[:, 1:2] * one + taps[:, 2:3] * two
            out_ref[f] = mixed.astype(out_ref.dtype)


def tail(where, behind, queries, c_mine, c_other, p_mine, p_other, groups, groups_other, spots, taps):
    frames, _, tokens = queries.shape
    steps = frames + 2
    own = lambda f, w: (jnp.clip(f - 2, 0, frames - 1), 0, 0)
    tile = lambda f: jnp.maximum(f - steps, 0)
    chunk = pl.BlockSpec((1, CHUNK, LANES), own)
    whole = pl.BlockSpec((2, CHUNK, LANES), lambda f, w: (0, 0, 0))
    pairs = sum(len(places) for places in spots)
    return pl.pallas_call(
        functools.partial(tail_kernel, spots),
        out_shape=jax.ShapeDtypeStruct((frames, D, tokens), jnp.bfloat16),
        grid_spec=pltpu.PrefetchScalarGridSpec(
            num_scalar_prefetch=1,
            grid=(steps + 2 * HALF_COLS // COL_TILE,),
            in_specs=[
                pl.BlockSpec((1, D, tokens), lambda f, w: (jnp.minimum(f, 1), 0, 0)),
                pl.BlockSpec((1, D, tokens), own),
            ]
            + [chunk] * 8
            + [whole] * 8
            + [pl.BlockSpec(memory_space=pl.ANY)] * (2 * len(groups))
            + [pl.BlockSpec((3, COL_TILE), lambda f, w: (0, tile(f)))],
            out_specs=pl.BlockSpec((frames, COL_TILE, tokens), lambda f, w: (0, tile(f), 0)),
            scratch_shapes=[
                pltpu.VMEM((2, HALF_ROWS, LANES), jnp.bfloat16),
                pltpu.VMEM((D, tokens), jnp.bfloat16),
                pltpu.VMEM((2 * HALF_ROWS, steps * tokens), jnp.bfloat16),
                pltpu.VMEM((2 * HALF_ROWS, 2 * HALF_COLS), jnp.bfloat16),
                pltpu.SemaphoreType.DMA((2 * pairs,)),
            ],
        ),
        compiler_params=limit(40),
        cost_estimate=pl.CostEstimate(
            flops=2 * steps * tokens * D * (D + LANES), bytes_accessed=2 * D * D, transcendentals=0
        ),
        name="tail",
    )(where, behind, queries, *c_mine, *c_other, *p_mine, *p_other, *groups, *groups_other, taps)


def layer(queries, keys, values, out_weight, conv_taps):
    nx, nz, ny = lax.axis_size("x"), lax.axis_size("z"), lax.axis_size("y")
    sections = nx * nz
    core, row = lax.axis_index("c"), lax.axis_index("y")
    place = jnp.stack([lax.axis_index("x"), lax.axis_index("z")])
    where = jnp.stack([core, row, lax.axis_index("x"), lax.axis_index("z")])
    queries, keys, values = (jnp.transpose(a, (0, 2, 1)) for a in (queries, keys, values))

    def along_y(value):
        return [shift(value, "y", s, ny) for s in range(1, ny)]

    def to_partner(arrays):
        return [shift(value, "c", 1, 2) for value in arrays]

    rows, cols = out_weight.shape
    padded = jnp.pad(out_weight, ((0, PADDED - rows), (0, 2 * HALF_COLS - cols)))
    block = lax.dynamic_slice_in_dim(padded, core * HALF_COLS, HALF_COLS, axis=1)
    partner = lax.ppermute(block, "z", [(i, i ^ 1) for i in range(nz)])
    halo = queries[-2:]
    over = lax.ppermute(
        halo, ("x", "z"), [(i * nz + nz - 1, i * nz + 2 * nz - 1) for i in range(nx - 1)]
    )
    mine, theirs = local_kv(jnp.reshape(core, (1,)), keys, values)
    theirs = shift(theirs, "c", 1, 2)
    pair = in_order(place, block, after(partner, mine))
    above, below = shift(pair, "z", 2, nz), shift(pair, "z", -2, nz)
    pair_up, pair_down = shift(pair, "x", 1, nx), shift(pair, "x", -1, nx)
    own, *pieces = split(jnp.reshape(row, (1,)), mine, theirs)
    received = [shift(pieces[s - 1], "y", s, ny) for s in range(1, ny)]

    last, cuts = total(own, received, sections)
    cuts = lax.all_to_all(cuts, ("x", "z"), 0, 0)

    below = after(below, last)
    far = shift(below, "z", -2, nz)
    sides = pack([below, after(above, last)])
    sides_up, sides_down = shift(sides, "x", 1, nx), shift(sides, "x", -1, nx)
    received = [shift(after(pieces[s + 2], last), "y", s, ny) for s in range(1, ny)]
    cuts = exclusive_scan(cuts)
    before = lax.all_to_all(cuts, ("x", "z"), 0, 0)
    far_up, far_down = shift(after(far, cuts), "x", 1, nx), shift(after(far, cuts), "x", -1, nx)
    sides_two = shift(after(sides_up, cuts), "x", 1, nx)
    pair_two = shift(after(pair_down, cuts), "x", -1, nx)
    halo = jnp.where(lax.axis_index("z") == nz - 1, after(over, cuts), halo)
    behind = shift(halo, "z", 1, nz)
    sums = rest(own, [after(r, cuts) for r in received], last)
    c_mine = [sums] + along_y(sums)
    early = to_partner([after(a, cuts) for a in (pair, pair_up, pair_down, sides)])

    before = join(before)
    p_mine = [before] + along_y(before)
    far_two = shift(after(far_down, before), "x", -1, nx)
    c_other = to_partner([after(a, before) for a in c_mine])
    middle = to_partner([after(a, before) for a in (far, sides_up, sides_down, far_up, far_down)])
    p_other = to_partner(p_mine)
    late = to_partner([after(a, before) for a in (pair_two, sides_two, far_two)])

    here, near, across = (0,), (-1, 1), (-2,)
    spots = [
        [(dx, dz) for dz in steps]
        for dx, steps in (
            (0, here), (1, here), (-1, here), (0, near),
            (0, across), (1, near), (-1, near), (1, across), (-1, across),
            (-2, here), (2, near), (-2, across),
        )
    ]
    groups = [
        pair, pair_up, pair_down, sides,
        far, sides_up, sides_down, far_up, far_down,
        pair_two, sides_two, far_two,
    ]
    out = tail(where, behind, queries, c_mine, c_other, p_mine, p_other, groups, early + middle + late, spots, conv_taps)
    return jnp.transpose(out, (0, 2, 1))


def solution(mesh):
    fine = Mesh(mesh.devices.reshape(4, 8, 4, 2), ("x", "z", "y", "c"))
    in_specs = (
        P(("x", "z"), ("y", "c"), None),
        P(("x", "z"), ("y", "c"), None),
        P(("x", "z"), ("y", "c"), None),
        P(("x", "z"), None),
        P(),
    )
    return jax.shard_map(layer, mesh=fine, in_specs=in_specs, out_specs=in_specs[0], check_vma=False)
```

```python
import functools

import jax
import jax.numpy as jnp
from jax import lax
from jax.experimental import pallas as pl
from jax.experimental.pallas import tpu as pltpu
from jax.sharding import Mesh, PartitionSpec as P


HEADS = 20
HEAD_DIM = 112
D = HEADS * HEAD_DIM
LANES = 128
HALF_HEADS = HEADS // 2
HALF_ROWS = 1152
BLOCK, PADDED = 70, 72
PAIR = 2 * PADDED
CHUNK = 288
HALF_COLS = 1152
COL_TILE = 256

stab_eps = 1e-06


def shift(value, axis, distance, size):
    return lax.ppermute(value, axis, [(i, (i + distance) % size) for i in range(size)])


def after(value, *others):
    return lax.optimization_barrier((value,) + others)[0]


def kv_kernel(core_ref, k_ref, v_ref, mine_ref, theirs_ref, acc_ref):
    frame = pl.program_id(0)
    core = core_ref[0]

    @pl.when(frame == 0)
    def _():
        acc_ref[...] = jnp.zeros_like(acc_ref)

    tokens = k_ref.shape[2]
    pad = jnp.zeros((LANES - HEAD_DIM, tokens), jnp.bfloat16)
    ones = (lax.broadcasted_iota(jnp.int32, (LANES, tokens), 0) == HEAD_DIM).astype(jnp.bfloat16)
    for head in range(HEADS):
        half, inner = divmod(head, HALF_HEADS)
        keys = jnp.maximum(k_ref[0, head * HEAD_DIM : (head + 1) * HEAD_DIM, :], 0)
        vals = v_ref[0, head * HEAD_DIM : (head + 1) * HEAD_DIM, :]
        left = jnp.concatenate([vals, keys], axis=1)
        right = jnp.concatenate([jnp.concatenate([keys, pad], axis=0), ones], axis=1)
        part = lax.dot_general(
            left, right, (((1,), (1,)), ((), ())), preferred_element_type=jnp.float32
        )
        rows = slice(inner * HEAD_DIM, (inner + 1) * HEAD_DIM)
        acc_ref[half, rows, :] = acc_ref[half, rows, :] + part
    norm = lax.broadcasted_iota(jnp.int32, (PADDED, LANES), 1) == HEAD_DIM
    for ref, half in ((mine_ref, core), (theirs_ref, 1 - core)):
        for pair in range(HALF_ROWS // PAIR):
            cuts = [
                jnp.where(norm, acc_ref[half, b * PADDED : (b + 1) * PADDED, :], acc_ref[half, b * BLOCK : b * BLOCK + PADDED, :])
                for b in (2 * pair, 2 * pair + 1)
            ]
            ref[0, pair * PAIR : (pair + 1) * PAIR, :] = jnp.concatenate(cuts, axis=0).astype(ref.dtype)


def limit(mib):
    return pltpu.CompilerParams(vmem_limit_bytes=mib << 20)


def local_kv(core, keys, values):
    frames, _, tokens = keys.shape
    spec = pl.BlockSpec((1, D, tokens), lambda f, c: (f, 0, 0))
    out = pl.BlockSpec((1, HALF_ROWS, LANES), lambda f, c: (f, 0, 0))
    return pl.pallas_call(
        kv_kernel,
        out_shape=[jax.ShapeDtypeStruct((frames, HALF_ROWS, LANES), jnp.bfloat16)] * 2,
        grid_spec=pltpu.PrefetchScalarGridSpec(
            num_scalar_prefetch=1,
            grid=(frames,),
            in_specs=[spec, spec],
            out_specs=[out, out],
            scratch_shapes=[pltpu.VMEM((2, HALF_ROWS, LANES), jnp.float32)],
        ),
        compiler_params=limit(60),
        cost_estimate=pl.CostEstimate(
            flops=4 * frames * tokens * D * LANES, bytes_accessed=4 * frames * tokens * D * 2, transcendentals=0
        ),
        name="local_kv",
    )(core, keys, values)


def split_kernel(row_ref, mine_ref, other_ref, own_ref, *piece_refs):
    frames = mine_ref.shape[0]
    for s in range(4):
        rows = pl.ds(pl.multiple_of(lax.rem(row_ref[0] + s, 4) * CHUNK, CHUNK), CHUNK)
        for f in range(frames):
            total = mine_ref[f, rows, :].astype(jnp.float32) + other_ref[f, rows, :].astype(jnp.float32)
            if s == 0:
                own_ref[f] = total
            elif f >= frames - 2:
                piece_refs[s - 1][f - frames + 2] = total.astype(jnp.bfloat16)
            else:
                piece_refs[s + 2][f] = total.astype(jnp.bfloat16)


def split(row, mine, other):
    frames = mine.shape[0]
    vmem = pl.BlockSpec(memory_space=pltpu.VMEM)
    return pl.pallas_call(
        split_kernel,
        out_shape=[jax.ShapeDtypeStruct((frames, CHUNK, LANES), jnp.float32)]
        + [jax.ShapeDtypeStruct((2, CHUNK, LANES), jnp.bfloat16)] * 3
        + [jax.ShapeDtypeStruct((frames - 2, CHUNK, LANES), jnp.bfloat16)] * 3,
        in_specs=[pl.BlockSpec(memory_space=pltpu.SMEM), vmem, vmem],
        out_specs=[vmem] * 7,
        compiler_params=limit(8),
        name="split",
    )(row, mine, other)


def total_kernel(own_ref, a_ref, b_ref, c_ref, sums_ref, pieces_ref):
    frames = own_ref.shape[0]
    count, rows, _ = pieces_ref.shape
    rows //= 2
    kept = []
    for f in range(2):
        total = own_ref[frames - 2 + f]
        for ref in (a_ref, b_ref, c_ref):
            total = total + ref[f].astype(jnp.float32)
        sums_ref[f] = total.astype(sums_ref.dtype)
        kept.append(total)
    earlier, last = kept
    for i in range(count):
        cut = slice(i * rows, (i + 1) * rows)
        both = jnp.concatenate([last[cut], earlier[cut]], axis=0)
        pieces_ref[i] = both.astype(pieces_ref.dtype)


def total(own, received, sections):
    vmem = pl.BlockSpec(memory_space=pltpu.VMEM)
    return pl.pallas_call(
        total_kernel,
        out_shape=[
            jax.ShapeDtypeStruct((2,) + own.shape[1:], jnp.bfloat16),
            jax.ShapeDtypeStruct((sections, 2 * CHUNK // sections, LANES), jnp.bfloat16),
        ],
        in_specs=[vmem] * 4,
        out_specs=[vmem] * 2,
        compiler_params=limit(8),
        name="total",
    )(own, *received)


def rest_kernel(own_ref, a_ref, b_ref, c_ref, last_ref, sums_ref):
    first = a_ref.shape[0]
    for f in range(first):
        total = own_ref[f]
        for ref in (a_ref, b_ref, c_ref):
            total = total + ref[f].astype(jnp.float32)
        sums_ref[f] = total.astype(sums_ref.dtype)
    for f in range(2):
        sums_ref[first + f] = last_ref[f]


def rest(own, received, last):
    vmem = pl.BlockSpec(memory_space=pltpu.VMEM)
    return pl.pallas_call(
        rest_kernel,
        out_shape=jax.ShapeDtypeStruct(own.shape, jnp.bfloat16),
        in_specs=[vmem] * 5,
        out_specs=vmem,
        compiler_params=limit(8),
        name="rest",
    )(own, *received, last)


def scan_kernel(in_ref, out_ref):
    count, rows, lanes = in_ref.shape
    rows //= 2
    before = jnp.zeros((rows, lanes), jnp.float32)
    before2 = before
    for i in range(count):
        out_ref[i] = jnp.concatenate([before, before2], axis=0).astype(out_ref.dtype)
        here = in_ref[i].astype(jnp.float32)
        before, before2 = before + here[:rows], before + here[rows:]


def exclusive_scan(value):
    vmem = pl.BlockSpec(memory_space=pltpu.VMEM)
    return pl.pallas_call(
        scan_kernel,
        out_shape=jax.ShapeDtypeStruct(value.shape, value.dtype),
        in_specs=[vmem],
        out_specs=vmem,
        compiler_params=limit(8),
        name="exclusive_scan",
    )(value)


def join_kernel(in_ref, out_ref):
    count, rows, _ = in_ref.shape
    rows //= 2
    pieces = [in_ref[i].astype(jnp.float32) for i in range(count)]
    for k in range(2):
        whole = jnp.concatenate([p[k * rows : (k + 1) * rows] for p in pieces], axis=0)
        out_ref[k] = whole.astype(out_ref.dtype)


def join(value):
    vmem = pl.BlockSpec(memory_space=pltpu.VMEM)
    return pl.pallas_call(
        join_kernel,
        out_shape=jax.ShapeDtypeStruct((2, CHUNK, LANES), value.dtype),
        in_specs=[vmem],
        out_specs=vmem,
        compiler_params=limit(8),
        name="join",
    )(value)


def pair_kernel(place_ref, mine_ref, other_ref, out_ref):
    @pl.when(place_ref[1] % 2 == 0)
    def _():
        out_ref[:PADDED] = mine_ref[...]
        out_ref[PADDED:] = other_ref[...]

    @pl.when(place_ref[1] % 2 == 1)
    def _():
        out_ref[:PADDED] = other_ref[...]
        out_ref[PADDED:] = mine_ref[...]


def in_order(place, mine, other):
    vmem = pl.BlockSpec(memory_space=pltpu.VMEM)
    return pl.pallas_call(
        pair_kernel,
        out_shape=jax.ShapeDtypeStruct((PAIR,) + mine.shape[1:], mine.dtype),
        in_specs=[pl.BlockSpec(memory_space=pltpu.SMEM), vmem, vmem],
        out_specs=vmem,
        compiler_params=limit(8),
        name="in_order",
    )(place, mine, other)


def pack_kernel(*refs):
    for i, ref in enumerate(refs[:-1]):
        refs[-1][i] = ref[...]


def pack(arrays):
    vmem = pl.BlockSpec(memory_space=pltpu.VMEM)
    return pl.pallas_call(
        pack_kernel,
        out_shape=jax.ShapeDtypeStruct((len(arrays),) + arrays[0].shape, arrays[0].dtype),
        in_specs=[vmem] * len(arrays),
        out_specs=vmem,
        compiler_params=limit(8),
        name="pack",
    )(*arrays)


def padded_row(row):
    return row + (PADDED - BLOCK) * (row // BLOCK)


def tail_kernel(spots, where_ref, *refs):
    qh_ref, q_ref = refs[:2]
    c_refs, p_refs = (refs[2:6], refs[6:10]), (refs[10:14], refs[14:18])
    count = len(spots)
    w_refs = (refs[18 : 18 + count], refs[18 + count : 18 + 2 * count])
    taps_ref, out_ref, state_ref, query_ref, att_ref, weight_ref, sem = refs[18 + 2 * count :]
    step = pl.program_id(0)
    core, row = where_ref[0], where_ref[1]
    frames, width, tokens = out_ref.shape
    steps = frames + 2

    def copies():
        made = []
        for which in range(2):
            column = pl.multiple_of((which ^ core) * HALF_COLS, HALF_COLS)
            for group, places in zip(w_refs[which], spots):
                for i, (dx, dz) in enumerate(places):
                    x = lax.rem(where_ref[2] - dx + 8, 4)
                    z = lax.rem(where_ref[3] // 2 - dz + 8, 4)
                    start = pl.multiple_of((x * 4 + z) * PAIR, PAIR)
                    target = weight_ref.at[pl.ds(start, PAIR), pl.ds(column, HALF_COLS)]
                    source = group if len(places) == 1 else group.at[i]
                    made.append(pltpu.make_async_copy(source, target, sem.at[len(made)]))
        return made

    @pl.when(step == 0)
    def _():
        for copy in copies():
            copy.start()

    @pl.when(step < steps)
    def _():
        before = jnp.where(step == 0, 1, 0)
        within = jnp.where(step >= 2, 1.0, 0.0)
        for which in range(2):
            half = which ^ core
            for s in range(4):
                chunk = lax.rem(row - s + 4, 4)
                state = p_refs[which][s][before].astype(jnp.float32)
                state = state + c_refs[which][s][0].astype(jnp.float32) * within
                start = pl.multiple_of(chunk * CHUNK, CHUNK)
                state_ref[half, pl.ds(start, CHUNK), :] = state.astype(state_ref.dtype)

    @pl.when(step < 2)
    def _():
        query_ref[...] = jnp.maximum(qh_ref[0], 0)

    @pl.when((step >= 2) & (step < steps))
    def _():
        query_ref[...] = jnp.maximum(q_ref[0], 0)

    @pl.when(step < steps)
    def _():
        pad = jnp.zeros((LANES - HEAD_DIM, tokens), jnp.bfloat16)
        lanes = pl.ds(pl.multiple_of(step * tokens, tokens), tokens)
        for head in range(HEADS):
            half, inner = divmod(head, HALF_HEADS)
            query = query_ref[head * HEAD_DIM : (head + 1) * HEAD_DIM, :]
            first = padded_row(inner * HEAD_DIM)
            low = first // 16 * 16
            high = -(-(padded_row(inner * HEAD_DIM + HEAD_DIM - 1) + 1) // 16) * 16
            top = jnp.dot(
                state_ref[half, low:high, :],
                jnp.concatenate([query, pad], axis=0),
                preferred_element_type=jnp.float32,
            )
            norm = state_ref[half, inner * HEAD_DIM : (inner + 1) * HEAD_DIM, HEAD_DIM : HEAD_DIM + 1]
            bottom = norm.astype(jnp.float32) * query.astype(jnp.float32)
            bottom = jnp.sum(bottom, axis=0, keepdims=True) + stab_eps
            result = top * (1.0 / bottom)
            base = half * HALF_ROWS
            if first > low:
                held = att_ref[base + low : base + low + 16, lanes].astype(jnp.float32)
                keep = lax.broadcasted_iota(jnp.int32, (16, tokens), 0) < first - low
                att_ref[base + low : base + low + 16, lanes] = jnp.where(keep, held, result[:16]).astype(att_ref.dtype)
                att_ref[base + low + 16 : base + high, lanes] = result[16:].astype(att_ref.dtype)
            else:
                att_ref[base + low : base + high, lanes] = result.astype(att_ref.dtype)

    @pl.when(step == steps)
    def _():
        for copy in copies():
            copy.wait()

    @pl.when(step >= steps)
    def _():
        column = pl.ds(pl.multiple_of((step - steps) * width, width), width)
        prod = lax.dot_general(
            weight_ref[:, column], att_ref[...], (((0,), (0,)), ((), ())), preferred_element_type=jnp.float32
        )
        prod = prod.astype(jnp.bfloat16).astype(jnp.float32)
        taps = taps_ref[...].T
        for f in range(frames):
            now, one, two = (prod[:, (f + 2 - lag) * tokens : (f + 3 - lag) * tokens] for lag in range(3))
            mixed = taps[:, 0:1] * now + taps[:, 1:2] * one + taps[:, 2:3] * two
            out_ref[f] = mixed.astype(out_ref.dtype)


def tail(where, behind, queries, c_mine, c_other, p_mine, p_other, groups, groups_other, spots, taps):
    frames, _, tokens = queries.shape
    steps = frames + 2
    own = lambda f, w: (jnp.clip(f - 2, 0, frames - 1), 0, 0)
    tile = lambda f: jnp.maximum(f - steps, 0)
    chunk = pl.BlockSpec((1, CHUNK, LANES), own)
    whole = pl.BlockSpec((2, CHUNK, LANES), lambda f, w: (0, 0, 0))
    pairs = sum(len(places) for places in spots)
    return pl.pallas_call(
        functools.partial(tail_kernel, spots),
        out_shape=jax.ShapeDtypeStruct((frames, D, tokens), jnp.bfloat16),
        grid_spec=pltpu.PrefetchScalarGridSpec(
            num_scalar_prefetch=1,
            grid=(steps + 2 * HALF_COLS // COL_TILE,),
            in_specs=[
                pl.BlockSpec((1, D, tokens), lambda f, w: (jnp.minimum(f, 1), 0, 0)),
                pl.BlockSpec((1, D, tokens), own),
            ]
            + [chunk] * 8
            + [whole] * 8
            + [pl.BlockSpec(memory_space=pl.ANY)] * (2 * len(groups))
            + [pl.BlockSpec((3, COL_TILE), lambda f, w: (0, tile(f)))],
            out_specs=pl.BlockSpec((frames, COL_TILE, tokens), lambda f, w: (0, tile(f), 0)),
            scratch_shapes=[
                pltpu.VMEM((2, HALF_ROWS, LANES), jnp.bfloat16),
                pltpu.VMEM((D, tokens), jnp.bfloat16),
                pltpu.VMEM((2 * HALF_ROWS, steps * tokens), jnp.bfloat16),
                pltpu.VMEM((2 * HALF_ROWS, 2 * HALF_COLS), jnp.bfloat16),
                pltpu.SemaphoreType.DMA((2 * pairs,)),
            ],
        ),
        compiler_params=limit(40),
        cost_estimate=pl.CostEstimate(
            flops=2 * steps * tokens * D * (D + LANES), bytes_accessed=2 * D * D, transcendentals=0
        ),
        name="tail",
    )(where, behind, queries, *c_mine, *c_other, *p_mine, *p_other, *groups, *groups_other, taps)


def layer(queries, keys, values, out_weight, conv_taps):
    nx, nz, ny = lax.axis_size("x"), lax.axis_size("z"), lax.axis_size("y")
    sections = nx * nz
    core, row = lax.axis_index("c"), lax.axis_index("y")
    place = jnp.stack([lax.axis_index("x"), lax.axis_index("z")])
    where = jnp.stack([core, row, lax.axis_index("x"), lax.axis_index("z")])
    queries, keys, values = (jnp.transpose(a, (0, 2, 1)) for a in (queries, keys, values))

    def along_y(value):
        return [shift(value, "y", s, ny) for s in range(1, ny)]

    def to_partner(arrays):
        return [shift(value, "c", 1, 2) for value in arrays]

    rows, cols = out_weight.shape
    padded = jnp.pad(out_weight, ((0, PADDED - rows), (0, 2 * HALF_COLS - cols)))
    block = lax.dynamic_slice_in_dim(padded, core * HALF_COLS, HALF_COLS, axis=1)
    partner = lax.ppermute(block, "z", [(i, i ^ 1) for i in range(nz)])
    halo = queries[-2:]
    over = lax.ppermute(
        halo, ("x", "z"), [(i * nz + nz - 1, i * nz + 2 * nz - 1) for i in range(nx - 1)]
    )
    mine, theirs = local_kv(jnp.reshape(core, (1,)), keys, values)
    theirs = shift(theirs, "c", 1, 2)
    pair = in_order(place, block, after(partner, mine))
    above, below = shift(pair, "z", 2, nz), shift(pair, "z", -2, nz)
    pair_up, pair_down = shift(pair, "x", 1, nx), shift(pair, "x", -1, nx)
    own, *pieces = split(jnp.reshape(row, (1,)), mine, theirs)
    received = [shift(pieces[s - 1], "y", s, ny) for s in range(1, ny)]

    last, cuts = total(own, received, sections)
    cuts = lax.all_to_all(cuts, ("x", "z"), 0, 0)

    below = after(below, last)
    far = shift(below, "z", -2, nz)
    sides = pack([below, after(above, last)])
    sides_up, sides_down = shift(sides, "x", 1, nx), shift(sides, "x", -1, nx)
    received = [shift(after(pieces[s + 2], last), "y", s, ny) for s in range(1, ny)]
    cuts = exclusive_scan(cuts)
    before = lax.all_to_all(cuts, ("x", "z"), 0, 0)
    far_up, far_down = shift(after(far, cuts), "x", 1, nx), shift(after(far, cuts), "x", -1, nx)
    sides_two = shift(after(sides_up, cuts), "x", 1, nx)
    pair_two = shift(after(pair_down, cuts), "x", -1, nx)
    halo = jnp.where(lax.axis_index("z") == nz - 1, after(over, cuts), halo)
    behind = shift(halo, "z", 1, nz)
    sums = rest(own, [after(r, cuts) for r in received], last)
    c_mine = [sums] + along_y(sums)
    early = to_partner([after(a, cuts) for a in (pair, pair_up, pair_down, sides)])

    before = join(before)
    p_mine = [before] + along_y(before)
    far_two = shift(after(far_down, before), "x", -1, nx)
    c_other = to_partner([after(a, before) for a in c_mine])
    middle = to_partner([after(a, before) for a in (far, sides_up, sides_down, far_up, far_down)])
    p_other = to_partner(p_mine)
    late = to_partner([after(a, before) for a in (pair_two, sides_two, far_two)])

    here, near, across = (0,), (-1, 1), (-2,)
    spots = [
        [(dx, dz) for dz in steps]
        for dx, steps in (
            (0, here), (1, here), (-1, here), (0, near),
            (0, across), (1, near), (-1, near), (1, across), (-1, across),
            (-2, here), (2, near), (-2, across),
        )
    ]
    groups = [
        pair, pair_up, pair_down, sides,
        far, sides_up, sides_down, far_up, far_down,
        pair_two, sides_two, far_two,
    ]
    out = tail(where, behind, queries, c_mine, c_other, p_mine, p_other, groups, early + middle + late, spots, conv_taps)
    return jnp.transpose(out, (0, 2, 1))


def solution(mesh):
    fine = Mesh(mesh.devices.reshape(4, 8, 4, 2), ("x", "z", "y", "c"))
    in_specs = (
        P(("x", "z"), ("y", "c"), None),
        P(("x", "z"), ("y", "c"), None),
        P(("x", "z"), ("y", "c"), None),
        P(("x", "z"), None),
        P(),
    )
    return jax.shard_map(layer, mesh=fine, in_specs=in_specs, out_specs=in_specs[0], check_vma=False)
```
